32 devices in a mesh: row: 4 (over y, x), col: 8 (over z, core).
Axes of the slice: x: 2, y: 2, z: 4, core: 2. Of those that a mesh axis runs over, the one named last changes fastest.
Arguments:
- integrals: bfloat16 [2880, 23040], P('row', 'col'), may hold values from -0.0390625 to 0.0390625
- amplitudes: bfloat16 [23040, 256], P('col', 'row'), may hold values from -6 to 6
Outputs:
- ladder: bfloat16 [256, 2880], P('col', 'row')
The draws below stay inside these ranges and needn't reach their ends.
All inputs are finite; a program needn't handle non-finite values.
Results may differ from the reference program's by a relative error of at most 0.001.
Values may be sent and summed in bfloat16 or wider, within the bound.
A program may use at most 64 MiB of HBM per device.

```python
import jax
import jax.numpy as jnp
from jax import lax

AB = 2880
CD = 23040
PAIRS = 256


def steps_of(key, shape, pieces, least, largest):
    level, own = 1.0, jax.random.fold_in(key, 6)
    for axis_at, blocks in pieces:
        steps = jnp.exp(jax.random.uniform(jax.random.fold_in(own, axis_at), (blocks,), jnp.float32, least / len(pieces), largest / len(pieces)))
        level = level * jnp.repeat(steps, shape[axis_at] // blocks).reshape([-1 if axis == axis_at else 1 for axis in range(len(shape))])
    return level


def noise(own_key, dims, spread, most, pieces=(), held_as=jnp.bfloat16):
    entries = spread * jax.random.normal(own_key, dims, jnp.float32)
    if pieces:
        entries = entries * steps_of(own_key, dims, pieces, -0.22, 0.18)
    return jnp.clip(entries, -most, most).astype(held_as)


def setup_inputs(seed: int = 0) -> dict:
    splits = jax.random.split(jax.random.key(seed), 3)
    integrals = noise(splits[0], (AB, CD), CD ** -0.5, 0.0390625, ((0, 4), (1, 8)))
    amplitudes = noise(splits[1], (CD, PAIRS), 1.0, 6.0, ((0, 8), (1, 4)))
    return {"integrals": integrals, "amplitudes": amplitudes}


def reference(integrals, amplitudes):
    ladder_sum = lax.dot_general(amplitudes, integrals, (((0,), (1,)), ((), ())), preferred_element_type=jnp.float32)
    return ladder_sum.astype(jnp.bfloat16)
```

```python
import functools

import jax
import jax.numpy as jnp
from jax import lax
from jax.experimental import pallas as pl
from jax.experimental.pallas import tpu as pltpu
from jax.sharding import PartitionSpec as P

MESH = pl.DeviceIdType.MESH
NT = (((1,), (1,)), ((), ()))


def cuts_of(size, pieces, step):
    width = -(-size // (pieces * step)) * step
    return [(at, min(width, size - at)) for at in range(0, size, width)]


def ladder_kernel(chips, cuts, v_ref, t_ref, out_ref, v, t, parts, swap, summed, landed,
                  v_sem, t_sem, own_send, own_recv, far_send, far_recv,
                  swap_send, swap_recv, line_send, line_recv):
    half = t_ref.shape[0] // 2
    r, c = lax.axis_index("row"), lax.axis_index("col")
    z, core = c // 2, c % 2
    rx = r + 1 - 2 * (r % 2)
    ry = r + 2 - 4 * (r // 2)
    rd = 3 - r
    other = 1 - core

    def rows_of(h):
        return pl.ds(h * half, half)

    t_copy = pltpu.make_async_copy(t_ref, t.at[0], t_sem)
    t_copy.start()
    v_copies = []
    for i, (at, width) in enumerate(cuts):
        copy = pltpu.make_async_copy(v_ref.at[:, pl.ds(at, width)], v.at[:, pl.ds(at, width)], v_sem.at[i])
        copy.start()
        v_copies.append(copy)

    barrier = pltpu.get_barrier_semaphore()
    pl.semaphore_signal(barrier, inc=1, device_id={"row": rx}, device_id_type=MESH)
    pl.semaphore_signal(barrier, inc=1, device_id={"row": ry}, device_id_type=MESH)
    pl.semaphore_signal(barrier, inc=1, device_id={"col": 2 * z + other}, device_id_type=MESH)
    for step in range(1, chips):
        peer = lax.rem(z + step, chips)
        pl.semaphore_signal(barrier, inc=1, device_id={"col": 2 * peer + core}, device_id_type=MESH)
    pl.semaphore_wait(barrier, chips + 2)

    own = []
    for i, (h, slot, to) in enumerate(((0, 1, rx), (1, 1, ry), (1, 2, rx), (0, 2, ry))):
        copy = pltpu.make_async_remote_copy(
            src_ref=t_ref.at[rows_of(h)], dst_ref=t.at[slot, rows_of(h)],
            send_sem=own_send.at[i], recv_sem=own_recv.at[i], device_id={"row": to}, device_id_type=MESH)
        copy.start()
        own.append(copy)

    def multiply(slot, at, width):
        return lax.dot_general(t[slot, :, at:at + width], v[:, at:at + width], NT, preferred_element_type=jnp.float32)

    def swap_start(slot):
        copy = pltpu.make_async_remote_copy(
            src_ref=parts.at[slot, rows_of(other)], dst_ref=swap.at[slot],
            send_sem=swap_send.at[slot], recv_sem=swap_recv.at[slot],
            device_id={"col": 2 * z + other}, device_id_type=MESH)
        copy.start()
        return copy

    def goal(slot):
        first, second = ((r, r), (rx, ry), (ry, rx), (rd, rd))[slot]
        return first * other + second * core

    def line_copy(slot):
        return pltpu.make_async_remote_copy(
            src_ref=summed.at[slot], dst_ref=landed.at[z],
            send_sem=line_send.at[slot], recv_sem=line_recv.at[z],
            device_id={"col": 2 * goal(slot) + core}, device_id_type=MESH)

    def swap_finish(slot, copy):
        copy.wait_recv()
        total = parts[slot, rows_of(core)] + swap[slot]

        @pl.when(goal(slot) == z)
        def _():
            landed[z] = total

        @pl.when(goal(slot) != z)
        def _():
            summed[slot] = total
            line_copy(slot).start()

    t_copy.wait()
    for i, (at, width) in enumerate(cuts):
        v_copies[i].wait()
        term = multiply(0, at, width)
        parts[0] = term if i == 0 else parts[0] + term
    swaps = [swap_start(0)]

    own[0].wait_recv()
    own[1].wait_recv()
    far = []
    for i, (at, width) in enumerate(cuts):
        for h, to in ((0, ry), (1, rx)):
            where = (rows_of(h), pl.ds(at, width))
            copy = pltpu.make_async_remote_copy(
                src_ref=t.at[(1, *where)], dst_ref=t.at[(3, *where)],
                send_sem=far_send.at[i, h], recv_sem=far_recv.at[i, h], device_id={"row": to}, device_id_type=MESH)
            copy.start()
            far.append(copy)

    swap_finish(0, swaps[0])
    parts[1] = multiply(1, 0, t_ref.shape[1])
    swaps.append(swap_start(1))

    own[2].wait_recv()
    own[3].wait_recv()
    parts[2] = multiply(2, 0, t_ref.shape[1])
    swaps.append(swap_start(2))
    swap_finish(1, swaps[1])
    swap_finish(2, swaps[2])

    for i, (at, width) in enumerate(cuts):
        far[2 * i].wait_recv()
        far[2 * i + 1].wait_recv()
        term = multiply(3, at, width)
        parts[3] = term if i == 0 else parts[3] + term
    swaps.append(swap_start(3))
    swap_finish(3, swaps[3])

    for source in range(chips):
        @pl.when(z != source)
        def _():
            pltpu.make_async_copy(landed.at[source], landed.at[source], line_recv.at[source]).wait()
    total = landed[0]
    for source in range(1, chips):
        total = total + landed[source]
    out_ref[...] = total.astype(out_ref.dtype)

    for copy in own + far + swaps:
        copy.wait_send()
    for slot in range(4):
        @pl.when(goal(slot) != z)
        def _():
            line_copy(slot).wait_send()


def ladder_on_chips(integrals, amplitudes):
    chips = lax.axis_size("col") // 2
    blocks = amplitudes.T
    pairs, depth = blocks.shape
    rows = integrals.shape[0]
    half = pairs // 2
    cuts = cuts_of(depth, 4, 256)
    f32 = jnp.float32
    dma = pltpu.SemaphoreType.DMA
    return pl.pallas_call(
        functools.partial(ladder_kernel, chips, cuts),
        out_shape=jax.ShapeDtypeStruct((half, rows), jnp.bfloat16),
        in_specs=[pl.BlockSpec(memory_space=pl.ANY)] * 2,
        out_specs=pl.BlockSpec(memory_space=pltpu.VMEM),
        scratch_shapes=[
            pltpu.VMEM((rows, depth), jnp.bfloat16),
            pltpu.VMEM((4, pairs, depth), jnp.bfloat16),
            pltpu.VMEM((4, pairs, rows), f32),
            pltpu.VMEM((4, half, rows), f32),
            pltpu.VMEM((4, half, rows), f32),
            pltpu.VMEM((chips, half, rows), f32),
            dma((len(cuts),)), dma,
            dma((4,)), dma((4,)),
            dma((len(cuts), 2)), dma((len(cuts), 2)),
            dma((4,)), dma((4,)),
            dma((4,)), dma((chips,)),
        ],
        compiler_params=pltpu.CompilerParams(
            collective_id=0, has_side_effects=True, vmem_limit_bytes=48 * 1024 * 1024),
    )(integrals, blocks)


def per_device(integrals, amplitudes):
    columns = lax.axis_size("col")
    if lax.axis_size("row") == 4 and columns == 8:
        return ladder_on_chips(integrals, amplitudes)
    gathered = lax.all_gather(amplitudes, "row", axis=1, tiled=True)
    product = lax.dot_general(
        gathered, integrals, (((0,), (1,)), ((), ())), preferred_element_type=jnp.float32)
    return lax.psum_scatter(product, "col", scatter_dimension=0, tiled=True).astype(jnp.bfloat16)


def solution(mesh):
    in_specs = (P("row", "col"), P("col", "row"))
    out_specs = P("col", "row")
    return jax.shard_map(
        per_device, mesh=mesh, in_specs=in_specs, out_specs=out_specs, check_vma=False
    )
```

```python
import functools

import jax
import jax.numpy as jnp
from jax import lax
from jax.experimental import pallas as pl
from jax.experimental.pallas import tpu as pltpu
from jax.sharding import PartitionSpec as P

MESH = pl.DeviceIdType.MESH
NT = (((1,), (1,)), ((), ()))


def cuts_of(size, pieces, step):
    width = -(-size // (pieces * step)) * step
    return [(at, min(width, size - at)) for at in range(0, size, width)]


def ladder_kernel(chips, cuts, v_ref, t_ref, out_ref, v, t, parts, swap, summed, landed,
                  v_sem, t_sem, near_send, near_recv, far_send, far_recv, late_send, late_recv, last_send, last_recv,
                  swap_send, swap_recv, line_send, line_recv):
    depth = t_ref.shape[1]
    half = t_ref.shape[0] // 2
    part = half // 2
    r, c = lax.axis_index("row"), lax.axis_index("col")
    z, core = c // 2, c % 2
    rx = r + 1 - 2 * (r % 2)
    ry = r + 2 - 4 * (r // 2)
    rd = 3 - r
    other = 1 - core
    own = (0, half, (r, r), 0)
    near = (2 * half, half, (rx, ry), 0)
    far = [(4 * half + 4 * part * j, part, (rd, rd), part * j) for j in range(2)]
    late = [(4 * half + 4 * part * j + 2 * part, part, (ry, rx), part * j) for j in range(2)]
    slots = [own, near, far[0], late[0], far[1], late[1]]

    t_copy = pltpu.make_async_copy(t_ref, t.at[pl.ds(0, 2 * half)], t_sem)
    t_copy.start()
    v_copies = []
    for i, (at, width) in enumerate(cuts):
        copy = pltpu.make_async_copy(v_ref.at[:, pl.ds(at, width)], v.at[:, pl.ds(at, width)], v_sem.at[i])
        copy.start()
        v_copies.append(copy)

    barrier = pltpu.get_barrier_semaphore()
    pl.semaphore_signal(barrier, inc=1, device_id={"row": rx}, device_id_type=MESH)
    pl.semaphore_signal(barrier, inc=1, device_id={"row": ry}, device_id_type=MESH)
    pl.semaphore_signal(barrier, inc=1, device_id={"col": 2 * z + other}, device_id_type=MESH)
    for step in range(1, chips):
        peer = lax.rem(z + step, chips)
        pl.semaphore_signal(barrier, inc=1, device_id={"col": 2 * peer + core}, device_id_type=MESH)
    pl.semaphore_wait(barrier, chips + 2)

    def send(source, target, to, sems):
        copy = pltpu.make_async_remote_copy(
            src_ref=source, dst_ref=target, send_sem=sems[0], recv_sem=sems[1],
            device_id={"row": to}, device_id_type=MESH)
        copy.start()
        return copy

    def at_rows(first, count):
        return t.at[pl.ds(first, count)]

    near_copies = []
    for j in range(2):
        for h, to in ((0, rx), (1, ry)):
            near_copies.append(send(
                t_ref.at[pl.ds(h * half + j * part, part)], at_rows(near[0] + h * half + j * part, part), to,
                (near_send.at[j, h], near_recv.at[j, h])))

    def relay(j):
        copies = []
        for h, to in ((0, ry), (1, rx)):
            copies.append(send(
                at_rows(near[0] + h * half + j * part, part), at_rows(far[j][0] + h * part, part), to,
                (far_send.at[j, h], far_recv.at[j, h])))
        return copies

    def multiply(slot, at, width, several=1):
        first, count = slot[0], 2 * slot[1] * several
        return lax.dot_general(
            t[first:first + count, at:at + width], v[:, at:at + width], NT, preferred_element_type=jnp.float32)

    def swap_start(i):
        first, count, _, _ = slots[i]
        copy = pltpu.make_async_remote_copy(
            src_ref=parts.at[pl.ds(first + other * count, count)], dst_ref=swap.at[pl.ds(first // 2, count)],
            send_sem=swap_send.at[i], recv_sem=swap_recv.at[i],
            device_id={"col": 2 * z + other}, device_id_type=MESH)
        copy.start()
        return copy

    def goal(i):
        one, two = slots[i][2]
        return one * other + two * core

    def line_copy(i):
        first, count, _, place = slots[i]
        return pltpu.make_async_remote_copy(
            src_ref=summed.at[pl.ds(first // 2, count)], dst_ref=landed.at[z, pl.ds(place, count)],
            send_sem=line_send.at[i], recv_sem=line_recv.at[z],
            device_id={"col": 2 * goal(i) + core}, device_id_type=MESH)

    def swap_finish(i, copy):
        first, count, _, place = slots[i]
        copy.wait_recv()
        total = parts[pl.ds(first + core * count, count)] + swap[first // 2:first // 2 + count]

        @pl.when(goal(i) == z)
        def _():
            landed[z, place:place + count] = total

        @pl.when(goal(i) != z)
        def _():
            summed[first // 2:first // 2 + count] = total
            line_copy(i).start()

    def store(i, value):
        first, count = slots[i][0], 2 * slots[i][1]
        parts[first:first + count] = value

    def wait(copies):
        for copy in copies:
            copy.wait_recv()

    t_copy.wait()
    total = None
    for i, (at, width) in enumerate(cuts):
        v_copies[i].wait()
        term = multiply(own, at, width)
        total = term if total is None else total + term
    store(0, total)
    swaps = [swap_start(0)]

    wait(near_copies[:2])
    far_copies = relay(0)
    late_copies = []
    for h, to in ((1, rx), (0, ry)):
        late_copies.append(send(
            t_ref.at[pl.ds(h * half, part)], at_rows(late[0][0] + h * part, part), to,
            (late_send.at[h], late_recv.at[h])))
    swap_finish(0, swaps[0])

    wait(near_copies[2:])
    far_copies += relay(1)
    last_copies = []
    for i, (at, width) in enumerate(cuts):
        for h, to in ((1, rx), (0, ry)):
            last_copies.append(send(
                t_ref.at[pl.ds(h * half + part, part), pl.ds(at, width)],
                t.at[pl.ds(late[1][0] + h * part, part), pl.ds(at, width)], to,
                (last_send.at[i, h], last_recv.at[i, h])))
    store(1, multiply(near, 0, depth))
    swaps.append(swap_start(1))

    wait(far_copies[:2])
    swap_finish(1, swaps[1])
    wait(late_copies)
    both = multiply(far[0], 0, depth, several=2)
    store(2, both[:2 * part])
    store(3, both[2 * part:])
    swaps.append(swap_start(2))
    swaps.append(swap_start(3))

    wait(far_copies[2:])
    store(4, multiply(far[1], 0, depth))
    swaps.append(swap_start(4))
    swap_finish(2, swaps[2])
    swap_finish(3, swaps[3])

    total = None
    for i, (at, width) in enumerate(cuts):
        wait(last_copies[2 * i:2 * i + 2])
        term = multiply(late[1], at, width)
        total = term if total is None else total + term
        if i == len(cuts) - 2:
            swap_finish(4, swaps[4])
    store(5, total)
    swaps.append(swap_start(5))
    swap_finish(5, swaps[5])

    for source in range(chips):
        @pl.when(z != source)
        def _():
            pltpu.make_async_copy(landed.at[source], landed.at[source], line_recv.at[source]).wait()
    total = landed[0]
    for source in range(1, chips):
        total = total + landed[source]
    out_ref[...] = total.astype(out_ref.dtype)

    for copy in near_copies + far_copies + late_copies + last_copies + swaps:
        copy.wait_send()
    for i in range(len(slots)):
        @pl.when(goal(i) != z)
        def _():
            line_copy(i).wait_send()


def ladder_on_chips(integrals, amplitudes):
    chips = lax.axis_size("col") // 2
    blocks = amplitudes.T
    pairs, depth = blocks.shape
    rows = integrals.shape[0]
    half = pairs // 2
    cuts = cuts_of(depth, 4, 256)
    f32 = jnp.float32
    dma = pltpu.SemaphoreType.DMA
    return pl.pallas_call(
        functools.partial(ladder_kernel, chips, cuts),
        out_shape=jax.ShapeDtypeStruct((half, rows), jnp.bfloat16),
        in_specs=[pl.BlockSpec(memory_space=pl.ANY)] * 2,
        out_specs=pl.BlockSpec(memory_space=pltpu.VMEM),
        scratch_shapes=[
            pltpu.VMEM((rows, depth), jnp.bfloat16),
            pltpu.VMEM((4 * pairs, depth), jnp.bfloat16),
            pltpu.VMEM((4 * pairs, rows), f32),
            pltpu.VMEM((2 * pairs, rows), f32),
            pltpu.VMEM((2 * pairs, rows), f32),
            pltpu.VMEM((chips, half, rows), f32),
            dma((len(cuts),)), dma,
            dma((2, 2)), dma((2, 2)),
            dma((2, 2)), dma((2, 2)),
            dma((2,)), dma((2,)),
            dma((len(cuts), 2)), dma((len(cuts), 2)),
            dma((6,)), dma((6,)),
            dma((6,)), dma((chips,)),
        ],
        compiler_params=pltpu.CompilerParams(
            collective_id=0, has_side_effects=True, vmem_limit_bytes=67043328),
    )(integrals, blocks)


def per_device(integrals, amplitudes):
    columns = lax.axis_size("col")
    if lax.axis_size("row") == 4 and columns == 8:
        return ladder_on_chips(integrals, amplitudes)
    gathered = lax.all_gather(amplitudes, "row", axis=1, tiled=True)
    product = lax.dot_general(
        gathered, integrals, (((0,), (1,)), ((), ())), preferred_element_type=jnp.float32)
    return lax.psum_scatter(product, "col", scatter_dimension=0, tiled=True).astype(jnp.bfloat16)


def solution(mesh):
    in_specs = (P("row", "col"), P("col", "row"))
    out_specs = P("col", "row")
    return jax.shard_map(
        per_device, mesh=mesh, in_specs=in_specs, out_specs=out_specs, check_vma=False
    )
```

```python
import functools

import jax
import jax.numpy as jnp
from jax import lax
from jax.experimental import pallas as pl
from jax.experimental.pallas import tpu as pltpu
from jax.sharding import PartitionSpec as P

MESH = pl.DeviceIdType.MESH
NT = (((1,), (1,)), ((), ()))


def cuts_of(size, pieces, step):
    width = -(-size // (pieces * step)) * step
    return [(at, min(width, size - at)) for at in range(0, size, width)]


def ladder_kernel(chips, cuts, v_ref, t_ref, out_ref, v, t, parts, swap, summed, landed,
                  v_sem, t_sem, near_send, near_recv, far_send, far_recv, late_send, late_recv, last_send, last_recv,
                  swap_send, swap_recv, line_send, line_recv):
    depth = t_ref.shape[1]
    half = t_ref.shape[0] // 2
    part = half // 2
    r, c = lax.axis_index("row"), lax.axis_index("col")
    z, core = c // 2, c % 2
    rx = r + 1 - 2 * (r % 2)
    ry = r + 2 - 4 * (r // 2)
    rd = 3 - r
    other = 1 - core
    own = (0, half, (r, r), 0)
    near = (2 * half, half, (rx, ry), 0)
    far = [(4 * half + 2 * part * j, part, (rd, rd), part * j) for j in range(2)]
    late = (6 * half, half, (ry, rx), 0)
    slots = [own, near, *far, late]

    t_copy = pltpu.make_async_copy(t_ref, t.at[pl.ds(0, 2 * half)], t_sem)
    t_copy.start()
    v_copies = []
    for i, (at, width) in enumerate(cuts):
        copy = pltpu.make_async_copy(v_ref.at[:, pl.ds(at, width)], v.at[:, pl.ds(at, width)], v_sem.at[i])
        copy.start()
        v_copies.append(copy)

    barrier = pltpu.get_barrier_semaphore()
    pl.semaphore_signal(barrier, inc=1, device_id={"row": rx}, device_id_type=MESH)
    pl.semaphore_signal(barrier, inc=1, device_id={"row": ry}, device_id_type=MESH)
    pl.semaphore_signal(barrier, inc=1, device_id={"col": 2 * z + other}, device_id_type=MESH)
    for step in range(1, chips):
        peer = lax.rem(z + step, chips)
        pl.semaphore_signal(barrier, inc=1, device_id={"col": 2 * peer + core}, device_id_type=MESH)
    pl.semaphore_wait(barrier, chips + 2)

    def send(source, target, to, sems):
        copy = pltpu.make_async_remote_copy(
            src_ref=source, dst_ref=target, send_sem=sems[0], recv_sem=sems[1],
            device_id={"row": to}, device_id_type=MESH)
        copy.start()
        return copy

    def at_rows(first, count):
        return t.at[pl.ds(first, count)]

    near_copies = []
    for j in range(2):
        for h, to in ((0, rx), (1, ry)):
            near_copies.append(send(
                t_ref.at[pl.ds(h * half + j * part, part)], at_rows(near[0] + h * half + j * part, part), to,
                (near_send.at[j, h], near_recv.at[j, h])))

    def relay(j):
        copies = []
        for h, to in ((0, ry), (1, rx)):
            copies.append(send(
                at_rows(near[0] + h * half + j * part, part), at_rows(far[j][0] + h * part, part), to,
                (far_send.at[j, h], far_recv.at[j, h])))
        return copies

    def multiply(slot, at, width):
        first, count = slot[0], 2 * slot[1]
        return lax.dot_general(
            t[first:first + count, at:at + width], v[:, at:at + width], NT, preferred_element_type=jnp.float32)

    def swap_start(i):
        first, count, _, _ = slots[i]
        copy = pltpu.make_async_remote_copy(
            src_ref=parts.at[pl.ds(first + other * count, count)], dst_ref=swap.at[pl.ds(first // 2, count)],
            send_sem=swap_send.at[i], recv_sem=swap_recv.at[i],
            device_id={"col": 2 * z + other}, device_id_type=MESH)
        copy.start()
        return copy

    def goal(i):
        one, two = slots[i][2]
        return one * other + two * core

    def line_copy(i):
        first, count, _, place = slots[i]
        return pltpu.make_async_remote_copy(
            src_ref=summed.at[pl.ds(first // 2, count)], dst_ref=landed.at[z, pl.ds(place, count)],
            send_sem=line_send.at[i], recv_sem=line_recv.at[z],
            device_id={"col": 2 * goal(i) + core}, device_id_type=MESH)

    def swap_finish(i, copy):
        first, count, _, place = slots[i]
        copy.wait_recv()
        total = parts[pl.ds(first + core * count, count)] + swap[first // 2:first // 2 + count]

        @pl.when(goal(i) == z)
        def _():
            landed[z, place:place + count] = total

        @pl.when(goal(i) != z)
        def _():
            summed[first // 2:first // 2 + count] = total
            line_copy(i).start()

    def store(i, value):
        first, count = slots[i][0], 2 * slots[i][1]
        parts[first:first + count] = value

    def wait(copies):
        for copy in copies:
            copy.wait_recv()

    t_copy.wait()
    total = None
    for i, (at, width) in enumerate(cuts):
        v_copies[i].wait()
        term = multiply(own, at, width)
        total = term if total is None else total + term
    store(0, total)
    swaps = [swap_start(0)]

    wait(near_copies[:2])
    far_copies = relay(0)
    swap_finish(0, swaps[0])
    wait(near_copies[2:])
    far_copies += relay(1)
    late_copies = []
    for h, to in ((1, rx), (0, ry)):
        late_copies.append(send(
            t_ref.at[pl.ds(h * half, part)], at_rows(late[0] + h * half, part), to,
            (late_send.at[h], late_recv.at[h])))
    last_copies = []
    for i, (at, width) in enumerate(cuts):
        for h, to in ((1, rx), (0, ry)):
            last_copies.append(send(
                t_ref.at[pl.ds(h * half + part, part), pl.ds(at, width)],
                t.at[pl.ds(late[0] + h * half + part, part), pl.ds(at, width)], to,
                (last_send.at[i, h], last_recv.at[i, h])))
    store(1, multiply(near, 0, depth))
    swaps.append(swap_start(1))

    wait(far_copies[:2])
    store(2, multiply(far[0], 0, depth))
    swaps.append(swap_start(2))
    swap_finish(1, swaps[1])

    wait(far_copies[2:])
    store(3, multiply(far[1], 0, depth))
    swaps.append(swap_start(3))
    swap_finish(2, swaps[2])

    wait(late_copies)
    total = None
    for i, (at, width) in enumerate(cuts):
        wait(last_copies[2 * i:2 * i + 2])
        term = multiply(late, at, width)
        total = term if total is None else total + term
        if i == 0:
            swap_finish(3, swaps[3])
    store(4, total)
    swaps.append(swap_start(4))
    swap_finish(4, swaps[4])

    for source in range(chips):
        @pl.when(z != source)
        def _():
            pltpu.make_async_copy(landed.at[source], landed.at[source], line_recv.at[source]).wait()
    total = landed[0]
    for source in range(1, chips):
        total = total + landed[source]
    out_ref[...] = total.astype(out_ref.dtype)

    for copy in near_copies + far_copies + late_copies + last_copies + swaps:
        copy.wait_send()
    for i in range(len(slots)):
        @pl.when(goal(i) != z)
        def _():
            line_copy(i).wait_send()


def ladder_on_chips(integrals, amplitudes):
    chips = lax.axis_size("col") // 2
    blocks = amplitudes.T
    pairs, depth = blocks.shape
    rows = integrals.shape[0]
    half = pairs // 2
    cuts = cuts_of(depth, 2, 256)
    f32 = jnp.float32
    dma = pltpu.SemaphoreType.DMA
    return pl.pallas_call(
        functools.partial(ladder_kernel, chips, cuts),
        out_shape=jax.ShapeDtypeStruct((half, rows), jnp.bfloat16),
        in_specs=[pl.BlockSpec(memory_space=pl.ANY)] * 2,
        out_specs=pl.BlockSpec(memory_space=pltpu.VMEM),
        scratch_shapes=[
            pltpu.VMEM((rows, depth), jnp.bfloat16),
            pltpu.VMEM((4 * pairs, depth), jnp.bfloat16),
            pltpu.VMEM((4 * pairs, rows), f32),
            pltpu.VMEM((2 * pairs, rows), f32),
            pltpu.VMEM((2 * pairs, rows), f32),
            pltpu.VMEM((chips, half, rows), f32),
            dma((len(cuts),)), dma,
            dma((2, 2)), dma((2, 2)),
            dma((2, 2)), dma((2, 2)),
            dma((2,)), dma((2,)),
            dma((len(cuts), 2)), dma((len(cuts), 2)),
            dma((5,)), dma((5,)),
            dma((5,)), dma((chips,)),
        ],
        compiler_params=pltpu.CompilerParams(
            collective_id=0, has_side_effects=True, vmem_limit_bytes=67043328),
    )(integrals, blocks)


def per_device(integrals, amplitudes):
    columns = lax.axis_size("col")
    if lax.axis_size("row") == 4 and columns == 8:
        return ladder_on_chips(integrals, amplitudes)
    gathered = lax.all_gather(amplitudes, "row", axis=1, tiled=True)
    product = lax.dot_general(
        gathered, integrals, (((0,), (1,)), ((), ())), preferred_element_type=jnp.float32)
    return lax.psum_scatter(product, "col", scatter_dimension=0, tiled=True).astype(jnp.bfloat16)


def solution(mesh):
    in_specs = (P("row", "col"), P("col", "row"))
    out_specs = P("col", "row")
    return jax.shard_map(
        per_device, mesh=mesh, in_specs=in_specs, out_specs=out_specs, check_vma=False
    )
```
